256 devices in a mesh: grp: 8 (over z_hi, core), blk: 32 (over x, y, z_lo).
Axes of the slice: x: 4, y: 4, z: 8 (z_hi: 4, z_lo: 2; z = z_hi * 2 + z_lo), core: 2. Of those that a mesh axis runs over, the one named last changes fastest.
Arguments:
- factors: bfloat16 [1024, 512, 512], P(('grp', 'blk')), may hold values from -6 to 6
- loadings: bfloat16 [512, 2048], replicated, may hold values from -0.25 to 0.25
- netload_map: bfloat16 [512, 200], replicated, may hold values from -0.25 to 0.25
- rule_weights: bfloat16 [32, 2048, 200], P('blk'), may hold values from -0.125 to 0.125
- rule_bias: float32 [32, 200], P('blk'), may hold values from -3 to 3
Outputs:
- decisions: bfloat16 [512, 1024, 200], P('blk', 'grp')
- rule_grad: float32 [32, 2048, 200], P('blk', 'grp')
The draws below stay inside these ranges and needn't reach their ends.
All inputs are finite; a program needn't handle non-finite values.
Results may differ from the reference program's by a relative error of at most 0.01.
Values may be sent and summed in bfloat16 or wider, within the bound.
A program may use at most 128 MiB of HBM per device.

```python
import math
import jax
import jax.numpy as jnp
from jax import lax

K = 512
F = 2048
REG = 200
HOUR_BLK = 16
PATHS = 1024
HOURS = 512
N_BLK = 32


def levels(own_key, shape, pieces, low, largest):
    def one(position, shards_of):
        heights = jax.random.uniform(jax.random.fold_in(jax.random.fold_in(own_key, 6), position), (shards_of,), jnp.float32, low / len(pieces), largest / len(pieces))
        return jnp.repeat(jnp.exp(heights), shape[position] // shards_of).reshape((-1,) + (1,) * (len(shape) - position - 1))

    level = one(*pieces[0])
    for cut in pieces[1:]:
        level = level * one(*cut)
    return level


def bell_draw(own_key, shape, spread, reach, split=(), held_as=jnp.bfloat16):
    result = spread * jax.random.normal(own_key, shape, jnp.float32)
    if split:
        result = result * levels(own_key, shape, split, -0.22, 0.18)
    return jnp.clip(result, -reach, reach).astype(held_as)


def setup_inputs(seed: int = 0) -> dict:
    streams_of = jax.random.split(jax.random.key(seed), 6)
    factors = bell_draw(streams_of[0], (PATHS, HOURS, K), 1.0, 6.0, ((0, 256),))
    loadings = bell_draw(streams_of[1], (K, F), K ** -0.5, 0.25)
    netload_map = bell_draw(streams_of[2], (K, REG), K ** -0.5, 0.25)
    rule_weights = bell_draw(streams_of[3], (N_BLK, F, REG), F ** -0.5, 0.125, ((0, 32),))
    rule_bias = bell_draw(streams_of[4], (N_BLK, REG), 0.5, 3.0, ((0, 32),), jnp.float32)
    return dict(factors=factors, loadings=loadings, netload_map=netload_map, rule_weights=rule_weights, rule_bias=rule_bias)


def reference(factors, loadings, netload_map, rule_weights, rule_bias):
    row_scale = 1.0 / math.sqrt(PATHS * HOUR_BLK)

    def one_block(index):
        start = index * HOUR_BLK
        shocks = lax.dynamic_slice_in_dim(factors, start, HOUR_BLK, 1)
        shocks = jnp.swapaxes(shocks, 0, 1).reshape(HOUR_BLK * PATHS, K)
        features = jnp.tanh(jnp.dot(shocks, loadings, preferred_element_type=jnp.float32)).astype(jnp.bfloat16)
        net_load = jnp.dot(shocks, netload_map, preferred_element_type=jnp.float32).astype(jnp.bfloat16)
        weights = lax.dynamic_index_in_dim(rule_weights, index, 0, keepdims=False)
        offsets = lax.dynamic_index_in_dim(rule_bias, index, 0, keepdims=False)
        dispatch = jnp.dot(features, weights, preferred_element_type=jnp.float32) + offsets
        shortfall = net_load.astype(jnp.float32) - dispatch
        slopes = (-4.0 * jax.nn.sigmoid(shortfall) + jax.nn.sigmoid(-shortfall) + 0.25 * dispatch).astype(jnp.bfloat16)
        grad_block = jnp.dot(features.T, slopes, preferred_element_type=jnp.float32) * row_scale
        return (dispatch.astype(jnp.bfloat16).reshape(HOUR_BLK, PATHS, REG), grad_block)
    decisions, grads = lax.map(one_block, jnp.arange(N_BLK, dtype=jnp.int32))
    return (decisions.reshape(HOURS, PATHS, REG), grads)
```

```python
import math

import jax
import jax.numpy as jnp
from jax import lax
from jax.sharding import PartitionSpec as P


def body(factors, loadings, netload_map, rule_weights, rule_bias):
    blocks = lax.axis_size("blk")
    groups = lax.axis_size("grp")
    path_dev, hours, width_k = factors.shape
    hour_blk = hours // blocks
    row_scale = 1.0 / math.sqrt(groups * blocks * path_dev * hour_blk)
    weights = rule_weights[0]
    offsets = rule_bias[0]
    ordered = factors.reshape(path_dev, blocks, hour_blk, width_k)
    shocks = lax.all_to_all(ordered, "blk", split_axis=1, concat_axis=0, tiled=True)
    shocks = shocks.reshape(blocks * path_dev, hour_blk, width_k)
    features = jnp.tanh(
        jnp.einsum("rkc,cf->rkf", shocks, loadings, preferred_element_type=jnp.float32)
    ).astype(jnp.bfloat16)
    net_load = jnp.einsum(
        "rkc,cd->rkd", shocks, netload_map, preferred_element_type=jnp.float32
    ).astype(jnp.bfloat16)
    dispatch = (
        jnp.einsum("rkf,fd->rkd", features, weights, preferred_element_type=jnp.float32)
        + offsets
    )
    shortfall = net_load.astype(jnp.float32) - dispatch
    slopes = (
        -4.0 * jax.nn.sigmoid(shortfall) + jax.nn.sigmoid(-shortfall) + 0.25 * dispatch
    ).astype(jnp.bfloat16)
    decisions = jnp.transpose(dispatch.astype(jnp.bfloat16), (1, 0, 2))
    partial_grad = (
        jnp.einsum("rkf,rkd->fd", features, slopes, preferred_element_type=jnp.float32) * row_scale
    ).astype(jnp.bfloat16)
    grad_share = lax.psum_scatter(partial_grad, "grp", scatter_dimension=0, tiled=True)
    return (decisions, grad_share.astype(jnp.float32)[None])


def solution(mesh):
    return jax.shard_map(
        body,
        mesh=mesh,
        in_specs=(P(("grp", "blk"), None, None), P(), P(), P("blk", None, None), P("blk", None)),
        out_specs=(P("blk", "grp", None), P("blk", "grp", None)),
        check_vma=False,
    )
```

```python
import functools
import math

import jax
import jax.numpy as jnp
from jax import lax
from jax.experimental import pallas as pl
from jax.experimental.pallas import tpu as pltpu
from jax.sharding import PartitionSpec as P

MESH = pl.DeviceIdType.MESH
GROUP = 4


def near_first(x, y, z):
    steps = [(dx, dy, dz) for dx in range(x) for dy in range(y) for dz in range(z)]
    return sorted(steps, key=lambda s: min(s[0], x - s[0]) + min(s[1], y - s[1]) + s[2])


def dot_nt(a, b):
    return lax.dot_general(a, b, (((1,), (1,)), ((), ())), preferred_element_type=jnp.float32)


def kernel(
    row_scale,
    f_ref, ld_ref, mp_ref, w_ref, b_ref,
    dec_ref, grad_ref,
    recv, ld, mp, w, bias, feats_a, feats_b, slopes_a, slopes_b, acc, disp, dec_buf,
    s1_send, s1_recv, s2_send, s2_recv, keep,
    load_sem, own_sem, a2a_send, a2a_recv, dec_sem, s1_sems, s1_rsems, s2_sems, s2_rsems,
):
    feats, slopes_t = (feats_a, feats_b), (slopes_a, slopes_b)
    blk = lax.axis_index("blk")
    grp = lax.axis_index("grp")
    path_dev, _, width_k = f_ref.shape
    blocks, _, hour_blk, _ = recv.shape
    share = path_dev * hour_blk
    width_f = ld_ref.shape[1]
    regions = mp_ref.shape[0]
    chunk = 256
    zh, core = grp // 2, grp % 2
    x, y, zl = blk // 8, (blk // 2) % 4, blk % 2
    steps = near_first(4, 4, 2)

    def across(step, sign):
        dx, dy, dz = step
        return (
            ((x + sign * dx + 4) % 4) * 8
            + ((y + sign * dy + 4) % 4) * 2
            + (1 - zl if dz else zl)
        )

    targets = [across(step, 1) for step in steps]
    sources = [across(step, -1) for step in steps]
    partner = (zh * 2 + 1 - core, blk)
    right = (((zh + 1) % 4) * 2 + core, blk)
    left = (((zh + 3) % 4) * 2 + core, blk)

    barrier = pltpu.get_barrier_semaphore()
    givers = [(grp, source) for source in sources[1:]] + [partner, right, left]
    for giver in givers:
        pl.semaphore_signal(barrier, inc=1, device_id=giver, device_id_type=MESH)

    def hours_of(owner):
        return f_ref.at[:, pl.ds(pl.multiple_of(owner * hour_blk, hour_blk), hour_blk), :]

    loads = [
        pltpu.make_async_copy(ld_ref, ld, load_sem.at[0]),
        pltpu.make_async_copy(mp_ref, mp, load_sem.at[1]),
        pltpu.make_async_copy(w_ref.at[0], w, load_sem.at[2]),
        pltpu.make_async_copy(b_ref, bias, load_sem.at[3]),
        pltpu.make_async_copy(hours_of(blk), recv.at[0], own_sem),
    ]
    for load in loads:
        load.start()
    acc[...] = jnp.zeros_like(acc)
    pl.semaphore_wait(barrier, len(givers))

    sends = [
        pltpu.make_async_remote_copy(
            src_ref=hours_of(targets[slot]),
            dst_ref=recv.at[slot],
            send_sem=a2a_send.at[slot],
            recv_sem=a2a_recv.at[slot],
            device_id=(grp, targets[slot]),
            device_id_type=MESH,
        )
        for slot in range(1, blocks)
    ]
    for send in sends:
        send.start()
    for load in loads:
        load.wait()

    def arrived(slot):
        pltpu.make_async_remote_copy(
            src_ref=recv.at[slot], dst_ref=recv.at[slot], send_sem=a2a_send.at[0],
            recv_sem=a2a_recv.at[slot], device_id=partner, device_id_type=MESH,
        ).wait_recv()

    rows = GROUP * share

    def grad_of(at, side):
        part = pl.ds(pl.multiple_of(at, chunk), chunk)
        return acc[:, part] + jnp.dot(
            slopes_t[side][...], feats[side][:, part], preferred_element_type=jnp.float32
        )

    def decide(first, places, side, add_last):
        shocks = recv[pl.ds(first, GROUP)].reshape(rows, width_k)
        for at in range(0, width_f, chunk):
            feats[side][:, at : at + chunk] = jnp.tanh(
                jnp.dot(shocks, ld[:, at : at + chunk], preferred_element_type=jnp.float32)
            ).astype(jnp.bfloat16)
        net = dot_nt(shocks, mp[...])
        dispatch = jnp.broadcast_to(bias[...], (rows, regions))
        for at in range(0, width_f, chunk):
            dispatch = dispatch + dot_nt(feats[side][:, at : at + chunk], w[:, at : at + chunk])
            if add_last:
                acc[:, at : at + chunk] = grad_of(at, 1 - side)
        for i, place in enumerate(places):
            at = pl.multiple_of(place * share, share)
            for col in range(0, regions, 128):
                width = min(128, regions - col)
                disp[col // 128, pl.ds(at, share), :width] = dispatch[
                    i * share : (i + 1) * share, col : col + width
                ]
        shortfall = net.astype(jnp.bfloat16).astype(jnp.float32) - dispatch
        slopes = -1.5 - 2.5 * jnp.tanh(0.5 * shortfall) + 0.25 * dispatch
        slopes_t[side][...] = slopes.T.astype(jnp.bfloat16)

    side = 0
    for first in range(0, blocks, GROUP):
        side = (first // GROUP) % 2
        for slot in range(max(first, 1), first + GROUP):
            arrived(slot)
        decide(first, sources[first : first + GROUP], side, first > 0)

    turns = (2, 1, 3, 0)

    def slice_of(turn, at):
        return grad_of(((zh + turn) % 4) * (2 * chunk) + at * chunk, side)

    swaps = []
    for k, turn in enumerate(turns):
        s1_send[k] = slice_of(turn, 1 - core).astype(jnp.bfloat16)
        swaps.append(
            pltpu.make_async_remote_copy(
                src_ref=s1_send.at[k], dst_ref=s1_recv.at[k], send_sem=s1_sems.at[k],
                recv_sem=s1_rsems.at[k], device_id=partner, device_id_type=MESH,
            )
        )
        swaps[k].start()

    def hop(slot, to):
        return pltpu.make_async_remote_copy(
            src_ref=s2_send.at[slot], dst_ref=s2_recv.at[slot], send_sem=s2_sems.at[slot],
            recv_sem=s2_rsems.at[slot], device_id=to, device_id_type=MESH,
        )

    half = chunk // 2
    moves = [hop(0, right), hop(1, left), hop(2, right), hop(3, right), hop(4, left), hop(5, left)]

    def summed(k):
        value = slice_of(turns[k], core)
        swaps[k].wait_recv()
        return value + s1_recv[k].astype(jnp.float32)

    far = summed(0)
    s2_send[0] = far[:, :half].astype(jnp.bfloat16)
    moves[0].start()
    s2_send[1] = far[:, half:].astype(jnp.bfloat16)
    moves[1].start()
    ahead = summed(1)
    s2_send[3] = ahead[:, half:].astype(jnp.bfloat16)
    moves[3].start()
    keep[0] = ahead[:, :half]
    behind = summed(2)
    s2_send[4] = behind[:, :half].astype(jnp.bfloat16)
    moves[4].start()
    keep[1] = behind[:, half:]
    mine = summed(3)
    keep[2] = mine[:, :half]
    keep[3] = mine[:, half:]

    for hour in range(hour_blk):
        for side in range(0, regions, 128):
            width = min(128, regions - side)
            of_hour = disp[side // 128, pl.ds(hour, blocks * path_dev, stride=hour_blk), :]
            dec_buf[hour, side : side + width] = of_hour.T[:width].astype(jnp.bfloat16)
    out = pltpu.make_async_copy(dec_buf, dec_ref, dec_sem)
    out.start()

    moves[0].wait_recv()
    s2_send[2] = (keep[0] + s2_recv[0].astype(jnp.float32)).astype(jnp.bfloat16)
    moves[2].start()
    moves[1].wait_recv()
    s2_send[5] = (keep[1] + s2_recv[1].astype(jnp.float32)).astype(jnp.bfloat16)
    moves[5].start()
    for k in range(2, 6):
        moves[k].wait_recv()
    for k in range(2):
        total = keep[2 + k] + s2_recv[2 + k].astype(jnp.float32) + s2_recv[4 + k].astype(jnp.float32)
        grad_ref[0, :, k * half : (k + 1) * half] = total * row_scale

    out.wait()
    for copy in sends + swaps + moves:
        copy.wait_send()


def body(factors, loadings, netload_map, rule_weights, rule_bias):
    blocks = lax.axis_size("blk")
    grps = lax.axis_size("grp")
    path_dev, hours, width_k = factors.shape
    width_f, regions = rule_weights.shape[1:]
    hour_blk = hours // blocks
    row_scale = 1.0 / math.sqrt(grps * blocks * path_dev * hour_blk)
    share = path_dev * hour_blk
    owned = width_f // grps
    bf16, f32 = jnp.bfloat16, jnp.float32
    anywhere = pl.BlockSpec(memory_space=pl.ANY)
    dma = pltpu.SemaphoreType.DMA
    decisions_t, grad_t = pl.pallas_call(
        functools.partial(kernel, row_scale),
        out_shape=(
            jax.ShapeDtypeStruct((hour_blk, regions, blocks * path_dev), bf16),
            jax.ShapeDtypeStruct((1, regions, owned), f32),
        ),
        in_specs=[anywhere] * 5,
        out_specs=(anywhere, pl.BlockSpec(memory_space=pltpu.VMEM)),
        scratch_shapes=[
            pltpu.VMEM((blocks, path_dev, hour_blk, width_k), bf16),
            pltpu.VMEM(loadings.shape, bf16),
            pltpu.VMEM((regions, width_k), bf16),
            pltpu.VMEM((regions, width_f), bf16),
            pltpu.VMEM((1, regions), f32),
            pltpu.VMEM((GROUP * share, width_f), bf16),
            pltpu.VMEM((GROUP * share, width_f), bf16),
            pltpu.VMEM((regions, GROUP * share), bf16),
            pltpu.VMEM((regions, GROUP * share), bf16),
            pltpu.VMEM((regions, width_f), f32),
            pltpu.VMEM((-(-regions // 128), blocks * share, 128), f32),
            pltpu.VMEM((hour_blk, regions, blocks * path_dev), bf16),
            pltpu.VMEM((4, regions, owned), bf16),
            pltpu.VMEM((4, regions, owned), bf16),
            pltpu.VMEM((6, regions, owned // 2), bf16),
            pltpu.VMEM((6, regions, owned // 2), bf16),
            pltpu.VMEM((4, regions, owned // 2), f32),
            dma((4,)),
            dma,
            dma((blocks,)),
            dma((blocks,)),
            dma,
            dma((4,)),
            dma((4,)),
            dma((6,)),
            dma((6,)),
        ],
        compiler_params=pltpu.CompilerParams(
            collective_id=0, has_side_effects=True, vmem_limit_bytes=56 * 1024 * 1024
        ),
        name="exchange_decide_reduce",
    )(factors, loadings, netload_map.T, jnp.swapaxes(rule_weights, 1, 2), rule_bias)
    return jnp.swapaxes(decisions_t, 1, 2), jnp.swapaxes(grad_t, 1, 2)


def solution(mesh):
    return jax.shard_map(
        body,
        mesh=mesh,
        in_specs=(P(("grp", "blk"), None, None), P(), P(), P("blk", None, None), P("blk", None)),
        out_specs=(P("blk", "grp", None), P("blk", "grp", None)),
        check_vma=False,
    )
```

```python
import functools
import math

import jax
import jax.numpy as jnp
from jax import lax
from jax.experimental import pallas as pl
from jax.experimental.pallas import tpu as pltpu
from jax.sharding import PartitionSpec as P

MESH = pl.DeviceIdType.MESH
GROUP = 4


STEPS = (
    (0, 0, 0), (0, 0, 1), (1, 0, 0), (3, 0, 0),
    (1, 0, 1), (1, 1, 0), (1, 3, 0), (2, 0, 0),
    (3, 0, 1), (3, 1, 0), (3, 3, 0), (1, 1, 1),
    (1, 3, 1), (2, 0, 1), (0, 1, 0), (0, 3, 0),
    (0, 1, 1), (0, 2, 0), (0, 3, 1), (2, 1, 0),
    (2, 3, 0), (3, 1, 1), (3, 3, 1), (0, 2, 1),
    (1, 2, 1), (2, 1, 1), (1, 2, 0), (3, 2, 0),
    (2, 2, 0), (2, 3, 1), (3, 2, 1), (2, 2, 1),
)


def hops(step):
    return min(step[0], 4 - step[0]) + min(step[1], 4 - step[1]) + step[2]


SEND_ORDER = sorted(range(1, len(STEPS)), key=lambda slot: (hops(STEPS[slot]), STEPS[slot]))


def dot_nt(a, b):
    return lax.dot_general(a, b, (((1,), (1,)), ((), ())), preferred_element_type=jnp.float32)


def kernel(
    row_scale,
    f_ref, ld_ref, mp_ref, w_ref, b_ref,
    dec_ref, grad_ref,
    recv, ld, mp, w, bias, feats_a, feats_b, slopes_a, slopes_b, acc, disp,
    s1_send, s1_recv, s2_send, s2_recv, keep,
    load_sem, own_sem, a2a_send, a2a_recv, s1_sems, s1_rsems, s2_sems, s2_rsems,
):
    feats, slopes_t = (feats_a, feats_b), (slopes_a, slopes_b)
    blk = lax.axis_index("blk")
    grp = lax.axis_index("grp")
    path_dev, _, width_k = f_ref.shape
    blocks, _, hour_blk, _ = recv.shape
    share = path_dev * hour_blk
    width_f = ld_ref.shape[1]
    regions = mp_ref.shape[0]
    chunk = 256
    zh, core = grp // 2, grp % 2
    x, y, zl = blk // 8, (blk // 2) % 4, blk % 2

    def across(step, sign):
        dx, dy, dz = step
        return (
            ((x + sign * dx + 4) % 4) * 8
            + ((y + sign * dy + 4) % 4) * 2
            + (1 - zl if dz else zl)
        )

    targets = [across(step, 1) for step in STEPS]
    sources = [across(step, -1) for step in STEPS]
    partner = (zh * 2 + 1 - core, blk)
    right = (((zh + 1) % 4) * 2 + core, blk)
    left = (((zh + 3) % 4) * 2 + core, blk)

    barrier = pltpu.get_barrier_semaphore()
    givers = [(grp, source) for source in sources[1:]] + [partner, right, left]
    for giver in givers:
        pl.semaphore_signal(barrier, inc=1, device_id=giver, device_id_type=MESH)

    def hours_of(owner):
        return f_ref.at[:, pl.ds(pl.multiple_of(owner * hour_blk, hour_blk), hour_blk), :]

    loads = [
        pltpu.make_async_copy(ld_ref, ld, load_sem.at[0]),
        pltpu.make_async_copy(mp_ref, mp, load_sem.at[1]),
        pltpu.make_async_copy(w_ref.at[0], w, load_sem.at[2]),
        pltpu.make_async_copy(b_ref, bias, load_sem.at[3]),
        pltpu.make_async_copy(hours_of(blk), recv.at[0], own_sem),
    ]
    for load in loads:
        load.start()
    acc[...] = jnp.zeros_like(acc)
    pl.semaphore_wait(barrier, len(givers))

    sends = {
        slot: pltpu.make_async_remote_copy(
            src_ref=hours_of(targets[slot]),
            dst_ref=recv.at[slot],
            send_sem=a2a_send.at[slot],
            recv_sem=a2a_recv.at[slot],
            device_id=(grp, targets[slot]),
            device_id_type=MESH,
        )
        for slot in SEND_ORDER
    }
    for slot in SEND_ORDER:
        sends[slot].start()
    for load in loads:
        load.wait()

    def arrived(slot):
        pltpu.make_async_remote_copy(
            src_ref=recv.at[slot], dst_ref=recv.at[slot], send_sem=a2a_send.at[0],
            recv_sem=a2a_recv.at[slot], device_id=partner, device_id_type=MESH,
        ).wait_recv()

    rows = GROUP * share

    def grad_of(at, side):
        part = pl.ds(pl.multiple_of(at, chunk), chunk)
        return acc[:, part] + jnp.dot(
            slopes_t[side][...], feats[side][:, part], preferred_element_type=jnp.float32
        )

    def decide(first, places, side, add_last):
        shocks = recv[pl.ds(first, GROUP)].reshape(rows, width_k)
        for at in range(0, width_f, chunk):
            feats[side][:, at : at + chunk] = jnp.tanh(
                jnp.dot(shocks, ld[:, at : at + chunk], preferred_element_type=jnp.float32)
            ).astype(jnp.bfloat16)
        net = dot_nt(shocks, mp[...])
        dispatch = jnp.broadcast_to(bias[...], (rows, regions))
        for at in range(0, width_f, chunk):
            dispatch = dispatch + dot_nt(feats[side][:, at : at + chunk], w[:, at : at + chunk])
            if add_last:
                acc[:, at : at + chunk] = grad_of(at, 1 - side)
        for i, place in enumerate(places):
            at = pl.multiple_of(place * share, share)
            for col in range(0, regions, 128):
                width = min(128, regions - col)
                disp[col // 128, pl.ds(at, share), :width] = dispatch[
                    i * share : (i + 1) * share, col : col + width
                ]
        shortfall = net.astype(jnp.bfloat16).astype(jnp.float32) - dispatch
        slopes = -1.5 - 2.5 * jnp.tanh(0.5 * shortfall) + 0.25 * dispatch
        slopes_t[side][...] = slopes.T.astype(jnp.bfloat16)

    side = 0
    for first in range(0, blocks, GROUP):
        side = (first // GROUP) % 2
        for slot in range(max(first, 1), first + GROUP):
            arrived(slot)
        decide(first, sources[first : first + GROUP], side, first > 0)

    turns = (2, 1, 3, 0)

    def slice_of(turn, at):
        return grad_of(((zh + turn) % 4) * (2 * chunk) + at * chunk, side)

    swaps = []
    for k, turn in enumerate(turns):
        s1_send[k] = slice_of(turn, 1 - core).astype(jnp.bfloat16)
        swaps.append(
            pltpu.make_async_remote_copy(
                src_ref=s1_send.at[k], dst_ref=s1_recv.at[k], send_sem=s1_sems.at[k],
                recv_sem=s1_rsems.at[k], device_id=partner, device_id_type=MESH,
            )
        )
        swaps[k].start()

    def hop(slot, to):
        return pltpu.make_async_remote_copy(
            src_ref=s2_send.at[slot], dst_ref=s2_recv.at[slot], send_sem=s2_sems.at[slot],
            recv_sem=s2_rsems.at[slot], device_id=to, device_id_type=MESH,
        )

    half = chunk // 2
    moves = [hop(0, right), hop(1, left), hop(2, right), hop(3, right), hop(4, left), hop(5, left)]

    def summed(k):
        value = slice_of(turns[k], core)
        swaps[k].wait_recv()
        return value + s1_recv[k].astype(jnp.float32)

    far = summed(0)
    s2_send[0] = far[:, :half].astype(jnp.bfloat16)
    moves[0].start()
    s2_send[1] = far[:, half:].astype(jnp.bfloat16)
    moves[1].start()
    ahead = summed(1)
    s2_send[3] = ahead[:, half:].astype(jnp.bfloat16)
    keep[0] = ahead[:, :half]
    behind = summed(2)
    s2_send[4] = behind[:, :half].astype(jnp.bfloat16)
    keep[1] = behind[:, half:]
    moves[0].wait_send()
    moves[3].start()
    moves[1].wait_send()
    moves[4].start()
    mine = summed(3)
    keep[2] = mine[:, :half]
    keep[3] = mine[:, half:]

    for hour in range(hour_blk):
        for side in range(0, regions, 128):
            width = min(128, regions - side)
            of_hour = disp[side // 128, pl.ds(hour, blocks * path_dev, stride=hour_blk), :]
            dec_ref[hour, side : side + width] = of_hour.T[:width].astype(jnp.bfloat16)

    moves[0].wait_recv()
    s2_send[2] = (keep[0] + s2_recv[0].astype(jnp.float32)).astype(jnp.bfloat16)
    moves[2].start()
    moves[1].wait_recv()
    s2_send[5] = (keep[1] + s2_recv[1].astype(jnp.float32)).astype(jnp.bfloat16)
    moves[5].start()
    for k in range(2, 6):
        moves[k].wait_recv()
    for k in range(2):
        total = keep[2 + k] + s2_recv[2 + k].astype(jnp.float32) + s2_recv[4 + k].astype(jnp.float32)
        grad_ref[0, :, k * half : (k + 1) * half] = total * row_scale

    for copy in list(sends.values()) + swaps + moves[2:]:
        copy.wait_send()


def write_out(dec_ref, grad_ref, dec_out, grad_out, sems):
    copies = [
        pltpu.make_async_copy(dec_ref, dec_out, sems.at[0]),
        pltpu.make_async_copy(grad_ref, grad_out, sems.at[1]),
    ]
    for copy in copies:
        copy.start()
    for copy in copies:
        copy.wait()


def body(factors, loadings, netload_map, rule_weights, rule_bias):
    blocks = lax.axis_size("blk")
    grps = lax.axis_size("grp")
    path_dev, hours, width_k = factors.shape
    width_f, regions = rule_weights.shape[1:]
    hour_blk = hours // blocks
    row_scale = 1.0 / math.sqrt(grps * blocks * path_dev * hour_blk)
    share = path_dev * hour_blk
    owned = width_f // grps
    bf16, f32 = jnp.bfloat16, jnp.float32
    anywhere = pl.BlockSpec(memory_space=pl.ANY)
    vmem = pl.BlockSpec(memory_space=pltpu.VMEM)
    dma = pltpu.SemaphoreType.DMA
    decisions_t, grad_t = pl.pallas_call(
        functools.partial(kernel, row_scale),
        out_shape=(
            pltpu.VMEM((hour_blk, regions, blocks * path_dev), bf16),
            pltpu.VMEM((1, regions, owned), f32),
        ),
        in_specs=[anywhere] * 5,
        out_specs=(vmem, vmem),
        scratch_shapes=[
            pltpu.VMEM((blocks, path_dev, hour_blk, width_k), bf16),
            pltpu.VMEM(loadings.shape, bf16),
            pltpu.VMEM((regions, width_k), bf16),
            pltpu.VMEM((regions, width_f), bf16),
            pltpu.VMEM((1, regions), f32),
            pltpu.VMEM((GROUP * share, width_f), bf16),
            pltpu.VMEM((GROUP * share, width_f), bf16),
            pltpu.VMEM((regions, GROUP * share), bf16),
            pltpu.VMEM((regions, GROUP * share), bf16),
            pltpu.VMEM((regions, width_f), f32),
            pltpu.VMEM((-(-regions // 128), blocks * share, 128), f32),
            pltpu.VMEM((4, regions, owned), bf16),
            pltpu.VMEM((4, regions, owned), bf16),
            pltpu.VMEM((6, regions, owned // 2), bf16),
            pltpu.VMEM((6, regions, owned // 2), bf16),
            pltpu.VMEM((4, regions, owned // 2), f32),
            dma((4,)),
            dma,
            dma((blocks,)),
            dma((blocks,)),
            dma((4,)),
            dma((4,)),
            dma((6,)),
            dma((6,)),
        ],
        compiler_params=pltpu.CompilerParams(
            collective_id=0, has_side_effects=True, vmem_limit_bytes=56 * 1024 * 1024
        ),
        name="exchange_decide_reduce",
    )(factors, loadings, netload_map.T, jnp.swapaxes(rule_weights, 1, 2), rule_bias)
    decisions_t, grad_t = pl.pallas_call(
        write_out,
        out_shape=(
            jax.ShapeDtypeStruct(decisions_t.shape, bf16),
            jax.ShapeDtypeStruct(grad_t.shape, f32),
        ),
        in_specs=[vmem, vmem],
        out_specs=(anywhere, anywhere),
        scratch_shapes=[dma((2,))],
        name="write_out",
    )(*(pltpu.with_memory_space_constraint(a, pltpu.VMEM) for a in (decisions_t, grad_t)))
    return jnp.swapaxes(decisions_t, 1, 2), jnp.swapaxes(grad_t, 1, 2)


def solution(mesh):
    return jax.shard_map(
        body,
        mesh=mesh,
        in_specs=(P(("grp", "blk"), None, None), P(), P(), P("blk", None, None), P("blk", None)),
        out_specs=(P("blk", "grp", None), P("blk", "grp", None)),
        check_vma=False,
    )
```

```python
import functools
import math

import jax
import jax.numpy as jnp
from jax import lax
from jax.experimental import pallas as pl
from jax.experimental.pallas import tpu as pltpu
from jax.sharding import PartitionSpec as P

MESH = pl.DeviceIdType.MESH
GROUP = 4


STEPS = (
    (0, 0, 0), (0, 0, 1), (1, 0, 0), (3, 0, 0),
    (1, 0, 1), (1, 1, 0), (1, 3, 0), (2, 0, 0),
    (3, 0, 1), (3, 1, 0), (3, 3, 0), (1, 1, 1),
    (1, 3, 1), (2, 0, 1), (0, 1, 0), (0, 3, 0),
    (0, 1, 1), (0, 2, 0), (0, 3, 1), (2, 1, 0),
    (2, 3, 0), (3, 1, 1), (3, 3, 1), (0, 2, 1),
    (1, 2, 1), (2, 1, 1), (1, 2, 0), (3, 2, 0),
    (2, 2, 0), (2, 3, 1), (3, 2, 1), (2, 2, 1),
)


def hops(step):
    return min(step[0], 4 - step[0]) + min(step[1], 4 - step[1]) + step[2]


SEND_ORDER = sorted(range(1, len(STEPS)), key=lambda slot: (hops(STEPS[slot]), STEPS[slot]))


def dot_nt(a, b):
    return lax.dot_general(a, b, (((1,), (1,)), ((), ())), preferred_element_type=jnp.float32)


def kernel(
    row_scale,
    f_ref, ld_ref, mp_ref, w_ref, b_ref,
    dec_ref, grad_ref,
    recv, ld, mp, w, bias, feats_a, feats_b, slopes_a, slopes_b, acc, disp,
    s1_send, s1_recv, s2_send, s2_recv, keep,
    rounds, load_sem, own_sem, a2a_send, a2a_recv, s1_sems, s1_rsems, s2_sems, s2_rsems,
):
    feats, slopes_t = (feats_a, feats_b), (slopes_a, slopes_b)
    blk = lax.axis_index("blk")
    grp = lax.axis_index("grp")
    path_dev, _, width_k = f_ref.shape
    blocks, _, hour_blk, _ = recv.shape
    share = path_dev * hour_blk
    width_f = ld_ref.shape[1]
    regions = mp_ref.shape[0]
    chunk = 256
    zh, core = grp // 2, grp % 2
    x, y, zl = blk // 8, (blk // 2) % 4, blk % 2

    def across(step, sign):
        dx, dy, dz = step
        return (
            ((x + sign * dx + 4) % 4) * 8
            + ((y + sign * dy + 4) % 4) * 2
            + (1 - zl if dz else zl)
        )

    partner = (zh * 2 + 1 - core, blk)
    right = (((zh + 1) % 4) * 2 + core, blk)
    left = (((zh + 3) % 4) * 2 + core, blk)

    barrier = pltpu.get_barrier_semaphore()
    around = [(grp, across(STEPS[slot], 1)) for slot in SEND_ORDER if hops(STEPS[slot]) == 1]
    greeted = around + [partner, right, left]
    for device in greeted:
        pl.semaphore_signal(barrier, inc=1, device_id=device, device_id_type=MESH)

    targets = [across(step, 1) for step in STEPS]
    sources = [across(step, -1) for step in STEPS]

    def hours_of(owner):
        return f_ref.at[:, pl.ds(pl.multiple_of(owner * hour_blk, hour_blk), hour_blk), :]

    loads = [
        pltpu.make_async_copy(ld_ref, ld, load_sem.at[0]),
        pltpu.make_async_copy(mp_ref, mp, load_sem.at[1]),
        pltpu.make_async_copy(w_ref.at[0], w, load_sem.at[2]),
        pltpu.make_async_copy(b_ref, bias, load_sem.at[3]),
        pltpu.make_async_copy(hours_of(blk), recv.at[0], own_sem),
    ]
    for load in loads:
        load.start()
    pl.semaphore_wait(barrier, len(greeted))

    sends = {
        slot: pltpu.make_async_remote_copy(
            src_ref=hours_of(targets[slot]),
            dst_ref=recv.at[slot],
            send_sem=a2a_send.at[slot],
            recv_sem=a2a_recv.at[slot],
            device_id=(grp, targets[slot]),
            device_id_type=MESH,
        )
        for slot in SEND_ORDER
    }
    farthest = hops(STEPS[SEND_ORDER[-1]])
    for reach in range(1, farthest + 1):
        if reach > 1:
            pl.semaphore_wait(rounds.at[reach], len(around))
        if reach < farthest:
            for device in around:
                pl.semaphore_signal(
                    rounds.at[reach + 1], inc=1, device_id=device, device_id_type=MESH
                )
        for slot in SEND_ORDER:
            if hops(STEPS[slot]) == reach:
                sends[slot].start()
    for load in loads:
        load.wait()

    def arrived(slot):
        pltpu.make_async_remote_copy(
            src_ref=recv.at[slot], dst_ref=recv.at[slot], send_sem=a2a_send.at[0],
            recv_sem=a2a_recv.at[slot], device_id=partner, device_id_type=MESH,
        ).wait_recv()

    rows = GROUP * share

    def grad_of(at, side, add=True):
        part = pl.ds(pl.multiple_of(at, chunk), chunk)
        value = jnp.dot(
            slopes_t[side][...], feats[side][:, part], preferred_element_type=jnp.float32
        )
        return acc[:, part] + value if add else value

    def decide(first, places, side, add):
        shocks = recv[pl.ds(first, GROUP)].reshape(rows, width_k)
        for at in range(0, width_f, chunk):
            feats[side][:, at : at + chunk] = jnp.tanh(
                jnp.dot(shocks, ld[:, at : at + chunk], preferred_element_type=jnp.float32)
            ).astype(jnp.bfloat16)
        net = dot_nt(shocks, mp[...])
        dispatch = jnp.broadcast_to(bias[...], (rows, regions))
        for at in range(0, width_f, chunk):
            dispatch = dispatch + dot_nt(feats[side][:, at : at + chunk], w[:, at : at + chunk])
            if add is not None:
                acc[:, at : at + chunk] = grad_of(at, 1 - side, add)
        for i, place in enumerate(places):
            at = pl.multiple_of(place * share, share)
            for col in range(0, regions, 128):
                width = min(128, regions - col)
                disp[col // 128, pl.ds(at, share), :width] = dispatch[
                    i * share : (i + 1) * share, col : col + width
                ]
        shortfall = net.astype(jnp.bfloat16).astype(jnp.float32) - dispatch
        slopes = -1.5 - 2.5 * jnp.tanh(0.5 * shortfall) + 0.25 * dispatch
        slopes_t[side][...] = slopes.T.astype(jnp.bfloat16)

    side = 0
    for first in range(0, blocks, GROUP):
        side = (first // GROUP) % 2
        for slot in range(max(first, 1), first + GROUP):
            arrived(slot)
        decide(first, sources[first : first + GROUP], side, first > GROUP if first else None)

    turns = (2, 1, 3, 0)

    def slice_of(turn, at):
        return grad_of(((zh + turn) % 4) * (2 * chunk) + at * chunk, side)

    swaps = []
    for k, turn in enumerate(turns):
        s1_send[k] = slice_of(turn, 1 - core).astype(jnp.bfloat16)
        swaps.append(
            pltpu.make_async_remote_copy(
                src_ref=s1_send.at[k], dst_ref=s1_recv.at[k], send_sem=s1_sems.at[k],
                recv_sem=s1_rsems.at[k], device_id=partner, device_id_type=MESH,
            )
        )
        swaps[k].start()

    def hop(slot, to):
        return pltpu.make_async_remote_copy(
            src_ref=s2_send.at[slot], dst_ref=s2_recv.at[slot], send_sem=s2_sems.at[slot],
            recv_sem=s2_rsems.at[slot], device_id=to, device_id_type=MESH,
        )

    half = chunk // 2
    moves = [hop(0, right), hop(1, left), hop(2, right), hop(3, right), hop(4, left), hop(5, left)]

    def summed(k):
        value = slice_of(turns[k], core)
        swaps[k].wait_recv()
        return value + s1_recv[k].astype(jnp.float32)

    far = summed(0)
    s2_send[0] = far[:, :half].astype(jnp.bfloat16)
    moves[0].start()
    s2_send[1] = far[:, half:].astype(jnp.bfloat16)
    moves[1].start()
    ahead = summed(1)
    s2_send[3] = ahead[:, half:].astype(jnp.bfloat16)
    keep[0] = ahead[:, :half]
    behind = summed(2)
    s2_send[4] = behind[:, :half].astype(jnp.bfloat16)
    keep[1] = behind[:, half:]
    moves[0].wait_send()
    moves[3].start()
    moves[1].wait_send()
    moves[4].start()
    mine = summed(3)
    keep[2] = mine[:, :half]
    keep[3] = mine[:, half:]

    for hour in range(hour_blk):
        for side in range(0, regions, 128):
            width = min(128, regions - side)
            of_hour = disp[side // 128, pl.ds(hour, blocks * path_dev, stride=hour_blk), :]
            dec_ref[hour, side : side + width] = of_hour.T[:width].astype(jnp.bfloat16)

    moves[0].wait_recv()
    s2_send[2] = (keep[0] + s2_recv[0].astype(jnp.float32)).astype(jnp.bfloat16)
    moves[2].start()
    moves[1].wait_recv()
    s2_send[5] = (keep[1] + s2_recv[1].astype(jnp.float32)).astype(jnp.bfloat16)
    moves[5].start()
    for k in range(2, 6):
        moves[k].wait_recv()
    for k in range(2):
        total = keep[2 + k] + s2_recv[2 + k].astype(jnp.float32) + s2_recv[4 + k].astype(jnp.float32)
        grad_ref[0, :, k * half : (k + 1) * half] = total * row_scale

    for copy in list(sends.values()) + swaps + moves[2:]:
        copy.wait_send()


def write_out(dec_ref, grad_ref, dec_out, grad_out, sems):
    copies = [
        pltpu.make_async_copy(dec_ref, dec_out, sems.at[0]),
        pltpu.make_async_copy(grad_ref, grad_out, sems.at[1]),
    ]
    for copy in copies:
        copy.start()
    for copy in copies:
        copy.wait()


def body(factors, loadings, netload_map, rule_weights, rule_bias):
    blocks = lax.axis_size("blk")
    grps = lax.axis_size("grp")
    path_dev, hours, width_k = factors.shape
    width_f, regions = rule_weights.shape[1:]
    hour_blk = hours // blocks
    row_scale = 1.0 / math.sqrt(grps * blocks * path_dev * hour_blk)
    share = path_dev * hour_blk
    owned = width_f // grps
    bf16, f32 = jnp.bfloat16, jnp.float32
    anywhere = pl.BlockSpec(memory_space=pl.ANY)
    vmem = pl.BlockSpec(memory_space=pltpu.VMEM)
    dma = pltpu.SemaphoreType.DMA
    decisions_t, grad_t = pl.pallas_call(
        functools.partial(kernel, row_scale),
        out_shape=(
            pltpu.VMEM((hour_blk, regions, blocks * path_dev), bf16),
            pltpu.VMEM((1, regions, owned), f32),
        ),
        in_specs=[anywhere] * 5,
        out_specs=(vmem, vmem),
        scratch_shapes=[
            pltpu.VMEM((blocks, path_dev, hour_blk, width_k), bf16),
            pltpu.VMEM(loadings.shape, bf16),
            pltpu.VMEM((regions, width_k), bf16),
            pltpu.VMEM((regions, width_f), bf16),
            pltpu.VMEM((1, regions), f32),
            pltpu.VMEM((GROUP * share, width_f), bf16),
            pltpu.VMEM((GROUP * share, width_f), bf16),
            pltpu.VMEM((regions, GROUP * share), bf16),
            pltpu.VMEM((regions, GROUP * share), bf16),
            pltpu.VMEM((regions, width_f), f32),
            pltpu.VMEM((-(-regions // 128), blocks * share, 128), f32),
            pltpu.VMEM((4, regions, owned), bf16),
            pltpu.VMEM((4, regions, owned), bf16),
            pltpu.VMEM((6, regions, owned // 2), bf16),
            pltpu.VMEM((6, regions, owned // 2), bf16),
            pltpu.VMEM((4, regions, owned // 2), f32),
            pltpu.SemaphoreType.REGULAR((6,)),
            dma((4,)),
            dma,
            dma((blocks,)),
            dma((blocks,)),
            dma((4,)),
            dma((4,)),
            dma((6,)),
            dma((6,)),
        ],
        compiler_params=pltpu.CompilerParams(
            collective_id=0, has_side_effects=True, vmem_limit_bytes=56 * 1024 * 1024
        ),
        name="exchange_decide_reduce",
    )(factors, loadings, netload_map.T, jnp.swapaxes(rule_weights, 1, 2), rule_bias)
    decisions_t, grad_t = pl.pallas_call(
        write_out,
        out_shape=(
            jax.ShapeDtypeStruct(decisions_t.shape, bf16),
            jax.ShapeDtypeStruct(grad_t.shape, f32),
        ),
        in_specs=[vmem, vmem],
        out_specs=(anywhere, anywhere),
        scratch_shapes=[dma((2,))],
        name="write_out",
    )(*(pltpu.with_memory_space_constraint(a, pltpu.VMEM) for a in (decisions_t, grad_t)))
    return jnp.swapaxes(decisions_t, 1, 2), jnp.swapaxes(grad_t, 1, 2)


def solution(mesh):
    return jax.shard_map(
        body,
        mesh=mesh,
        in_specs=(P(("grp", "blk"), None, None), P(), P(), P("blk", None, None), P("blk", None)),
        out_specs=(P("blk", "grp", None), P("blk", "grp", None)),
        check_vma=False,
    )
```

```python
import functools
import math

import jax
import jax.numpy as jnp
from jax import lax
from jax.experimental import pallas as pl
from jax.experimental.pallas import tpu as pltpu
from jax.sharding import PartitionSpec as P

MESH = pl.DeviceIdType.MESH
BATCHES = (4, 4, 4, 4, 4, 4, 4, 2, 2)


STEPS = (
    (0, 0, 0), (0, 0, 1), (1, 0, 0), (3, 0, 0),
    (1, 0, 1), (1, 1, 0), (1, 3, 0), (2, 0, 0),
    (3, 0, 1), (3, 1, 0), (3, 3, 0), (1, 1, 1),
    (1, 3, 1), (2, 0, 1), (0, 1, 0), (0, 3, 0),
    (0, 1, 1), (0, 2, 0), (0, 3, 1), (2, 1, 0),
    (2, 3, 0), (3, 1, 1), (3, 3, 1), (0, 2, 1),
    (1, 2, 1), (2, 1, 1), (1, 2, 0), (3, 2, 0),
    (2, 2, 0), (2, 3, 1), (3, 2, 1), (2, 2, 1),
)


def hops(step):
    return min(step[0], 4 - step[0]) + min(step[1], 4 - step[1]) + step[2]


SEND_ORDER = sorted(range(1, len(STEPS)), key=lambda slot: (hops(STEPS[slot]), STEPS[slot]))


def dot_nt(a, b):
    return lax.dot_general(a, b, (((1,), (1,)), ((), ())), preferred_element_type=jnp.float32)


def kernel(
    row_scale,
    f_ref, ld_ref, mp_ref, w_ref, b_ref,
    dec_ref, grad_ref,
    recv, ld, mp, w, bias, feats_a, feats_b, slopes_a, slopes_b, acc, disp,
    s1_send, s1_recv, s2_send, s2_recv, keep,
    rounds, load_sem, own_sem, a2a_send, a2a_recv, s1_sems, s1_rsems, s2_sems, s2_rsems,
):
    feats, slopes_t = (feats_a, feats_b), (slopes_a, slopes_b)
    blk = lax.axis_index("blk")
    grp = lax.axis_index("grp")
    path_dev, _, width_k = f_ref.shape
    blocks, _, hour_blk, _ = recv.shape
    share = path_dev * hour_blk
    width_f = ld_ref.shape[1]
    regions = mp_ref.shape[0]
    chunk = 256
    zh, core = grp // 2, grp % 2
    x, y, zl = blk // 8, (blk // 2) % 4, blk % 2

    def across(step, sign):
        dx, dy, dz = step
        return (
            ((x + sign * dx + 4) % 4) * 8
            + ((y + sign * dy + 4) % 4) * 2
            + (1 - zl if dz else zl)
        )

    partner = (zh * 2 + 1 - core, blk)
    right = (((zh + 1) % 4) * 2 + core, blk)
    left = (((zh + 3) % 4) * 2 + core, blk)

    barrier = pltpu.get_barrier_semaphore()
    around = [(grp, across(STEPS[slot], 1)) for slot in SEND_ORDER if hops(STEPS[slot]) == 1]
    greeted = around + [partner, right, left]
    for device in greeted:
        pl.semaphore_signal(barrier, inc=1, device_id=device, device_id_type=MESH)

    targets = [across(step, 1) for step in STEPS]
    sources = [across(step, -1) for step in STEPS]

    def hours_of(owner):
        return f_ref.at[:, pl.ds(pl.multiple_of(owner * hour_blk, hour_blk), hour_blk), :]

    loads = [
        pltpu.make_async_copy(ld_ref, ld, load_sem.at[0]),
        pltpu.make_async_copy(mp_ref, mp, load_sem.at[1]),
        pltpu.make_async_copy(w_ref.at[0], w, load_sem.at[2]),
        pltpu.make_async_copy(b_ref, bias, load_sem.at[3]),
        pltpu.make_async_copy(hours_of(blk), recv.at[0], own_sem),
    ]
    for load in loads:
        load.start()
    pl.semaphore_wait(barrier, len(greeted))

    sends = {
        slot: pltpu.make_async_remote_copy(
            src_ref=hours_of(targets[slot]),
            dst_ref=recv.at[slot],
            send_sem=a2a_send.at[slot],
            recv_sem=a2a_recv.at[slot],
            device_id=(grp, targets[slot]),
            device_id_type=MESH,
        )
        for slot in SEND_ORDER
    }
    farthest = hops(STEPS[SEND_ORDER[-1]])
    for reach in range(1, farthest + 1):
        if reach > 1:
            pl.semaphore_wait(rounds.at[reach], len(around))
        if reach < farthest:
            for device in around:
                pl.semaphore_signal(
                    rounds.at[reach + 1], inc=1, device_id=device, device_id_type=MESH
                )
        for slot in SEND_ORDER:
            if hops(STEPS[slot]) == reach:
                sends[slot].start()
    for load in loads:
        load.wait()

    def arrived(slot):
        pltpu.make_async_remote_copy(
            src_ref=recv.at[slot], dst_ref=recv.at[slot], send_sem=a2a_send.at[0],
            recv_sem=a2a_recv.at[slot], device_id=partner, device_id_type=MESH,
        ).wait_recv()


    def grad_of(at, side, rows, add=True):
        part = pl.ds(pl.multiple_of(at, chunk), chunk)
        value = jnp.dot(
            slopes_t[side][:, :rows], feats[side][:rows, part], preferred_element_type=jnp.float32
        )
        return acc[:, part] + value if add else value

    def decide(first, places, side, before, add):
        rows = len(places) * share
        shocks = recv[pl.ds(first, len(places))].reshape(rows, width_k)
        for at in range(0, width_f, chunk):
            feats[side][:rows, at : at + chunk] = jnp.tanh(
                jnp.dot(shocks, ld[:, at : at + chunk], preferred_element_type=jnp.float32)
            ).astype(jnp.bfloat16)
        net = dot_nt(shocks, mp[...])
        dispatch = jnp.broadcast_to(bias[...], (rows, regions))
        for at in range(0, width_f, chunk):
            dispatch = dispatch + dot_nt(feats[side][:rows, at : at + chunk], w[:, at : at + chunk])
            if before:
                acc[:, at : at + chunk] = grad_of(at, 1 - side, before, add)
        for i, place in enumerate(places):
            at = pl.multiple_of(place * share, share)
            for col in range(0, regions, 128):
                width = min(128, regions - col)
                disp[col // 128, pl.ds(at, share), :width] = dispatch[
                    i * share : (i + 1) * share, col : col + width
                ]
        shortfall = net.astype(jnp.bfloat16).astype(jnp.float32) - dispatch
        slopes = -1.5 - 2.5 * jnp.tanh(0.5 * shortfall) + 0.25 * dispatch
        slopes_t[side][:, :rows] = slopes.T.astype(jnp.bfloat16)

    first = 0
    for batch, count in enumerate(BATCHES):
        side = batch % 2
        for slot in range(max(first, 1), first + count):
            arrived(slot)
        before = BATCHES[batch - 1] * share if batch else 0
        decide(first, sources[first : first + count], side, before, batch > 1)
        first += count

    turns = (2, 1, 3, 0)

    def slice_of(turn, at):
        return grad_of(((zh + turn) % 4) * (2 * chunk) + at * chunk, side, BATCHES[-1] * share)

    swaps = []
    for k, turn in enumerate(turns):
        s1_send[k] = slice_of(turn, 1 - core).astype(jnp.bfloat16)
        swaps.append(
            pltpu.make_async_remote_copy(
                src_ref=s1_send.at[k], dst_ref=s1_recv.at[k], send_sem=s1_sems.at[k],
                recv_sem=s1_rsems.at[k], device_id=partner, device_id_type=MESH,
            )
        )
        swaps[k].start()

    def hop(slot, to):
        return pltpu.make_async_remote_copy(
            src_ref=s2_send.at[slot], dst_ref=s2_recv.at[slot], send_sem=s2_sems.at[slot],
            recv_sem=s2_rsems.at[slot], device_id=to, device_id_type=MESH,
        )

    half = chunk // 2
    moves = [hop(0, right), hop(1, left), hop(2, right), hop(3, right), hop(4, left), hop(5, left)]

    def summed(k):
        value = slice_of(turns[k], core)
        swaps[k].wait_recv()
        return value + s1_recv[k].astype(jnp.float32)

    far = summed(0)
    s2_send[0] = far[:, :half].astype(jnp.bfloat16)
    moves[0].start()
    s2_send[1] = far[:, half:].astype(jnp.bfloat16)
    moves[1].start()
    ahead = summed(1)
    s2_send[3] = ahead[:, half:].astype(jnp.bfloat16)
    keep[0] = ahead[:, :half]
    behind = summed(2)
    s2_send[4] = behind[:, :half].astype(jnp.bfloat16)
    keep[1] = behind[:, half:]
    moves[0].wait_send()
    moves[3].start()
    moves[1].wait_send()
    moves[4].start()
    mine = summed(3)
    keep[2] = mine[:, :half]
    keep[3] = mine[:, half:]

    for hour in range(hour_blk):
        for side in range(0, regions, 128):
            width = min(128, regions - side)
            of_hour = disp[side // 128, pl.ds(hour, blocks * path_dev, stride=hour_blk), :]
            dec_ref[hour, side : side + width] = of_hour.T[:width].astype(jnp.bfloat16)

    moves[0].wait_recv()
    s2_send[2] = (keep[0] + s2_recv[0].astype(jnp.float32)).astype(jnp.bfloat16)
    moves[2].start()
    moves[1].wait_recv()
    s2_send[5] = (keep[1] + s2_recv[1].astype(jnp.float32)).astype(jnp.bfloat16)
    moves[5].start()
    for k in range(2, 6):
        moves[k].wait_recv()
    for k in range(2):
        total = keep[2 + k] + s2_recv[2 + k].astype(jnp.float32) + s2_recv[4 + k].astype(jnp.float32)
        grad_ref[0, :, k * half : (k + 1) * half] = total * row_scale

    for copy in list(sends.values()) + swaps + moves[2:]:
        copy.wait_send()


def write_out(dec_ref, grad_ref, dec_out, grad_out, sems):
    copies = [
        pltpu.make_async_copy(dec_ref, dec_out, sems.at[0]),
        pltpu.make_async_copy(grad_ref, grad_out, sems.at[1]),
    ]
    for copy in copies:
        copy.start()
    for copy in copies:
        copy.wait()


def body(factors, loadings, netload_map, rule_weights, rule_bias):
    blocks = lax.axis_size("blk")
    grps = lax.axis_size("grp")
    path_dev, hours, width_k = factors.shape
    width_f, regions = rule_weights.shape[1:]
    hour_blk = hours // blocks
    row_scale = 1.0 / math.sqrt(grps * blocks * path_dev * hour_blk)
    share = path_dev * hour_blk
    owned = width_f // grps
    bf16, f32 = jnp.bfloat16, jnp.float32
    anywhere = pl.BlockSpec(memory_space=pl.ANY)
    vmem = pl.BlockSpec(memory_space=pltpu.VMEM)
    dma = pltpu.SemaphoreType.DMA
    decisions_t, grad_t = pl.pallas_call(
        functools.partial(kernel, row_scale),
        out_shape=(
            pltpu.VMEM((hour_blk, regions, blocks * path_dev), bf16),
            pltpu.VMEM((1, regions, owned), f32),
        ),
        in_specs=[anywhere] * 5,
        out_specs=(vmem, vmem),
        scratch_shapes=[
            pltpu.VMEM((blocks, path_dev, hour_blk, width_k), bf16),
            pltpu.VMEM(loadings.shape, bf16),
            pltpu.VMEM((regions, width_k), bf16),
            pltpu.VMEM((regions, width_f), bf16),
            pltpu.VMEM((1, regions), f32),
            pltpu.VMEM((max(BATCHES) * share, width_f), bf16),
            pltpu.VMEM((max(BATCHES) * share, width_f), bf16),
            pltpu.VMEM((regions, max(BATCHES) * share), bf16),
            pltpu.VMEM((regions, max(BATCHES) * share), bf16),
            pltpu.VMEM((regions, width_f), f32),
            pltpu.VMEM((-(-regions // 128), blocks * share, 128), f32),
            pltpu.VMEM((4, regions, owned), bf16),
            pltpu.VMEM((4, regions, owned), bf16),
            pltpu.VMEM((6, regions, owned // 2), bf16),
            pltpu.VMEM((6, regions, owned // 2), bf16),
            pltpu.VMEM((4, regions, owned // 2), f32),
            pltpu.SemaphoreType.REGULAR((6,)),
            dma((4,)),
            dma,
            dma((blocks,)),
            dma((blocks,)),
            dma((4,)),
            dma((4,)),
            dma((6,)),
            dma((6,)),
        ],
        compiler_params=pltpu.CompilerParams(
            collective_id=0, has_side_effects=True, vmem_limit_bytes=56 * 1024 * 1024
        ),
        name="exchange_decide_reduce",
    )(factors, loadings, netload_map.T, jnp.swapaxes(rule_weights, 1, 2), rule_bias)
    decisions_t, grad_t = pl.pallas_call(
        write_out,
        out_shape=(
            jax.ShapeDtypeStruct(decisions_t.shape, bf16),
            jax.ShapeDtypeStruct(grad_t.shape, f32),
        ),
        in_specs=[vmem, vmem],
        out_specs=(anywhere, anywhere),
        scratch_shapes=[dma((2,))],
        name="write_out",
    )(*(pltpu.with_memory_space_constraint(a, pltpu.VMEM) for a in (decisions_t, grad_t)))
    return jnp.swapaxes(decisions_t, 1, 2), jnp.swapaxes(grad_t, 1, 2)


def solution(mesh):
    return jax.shard_map(
        body,
        mesh=mesh,
        in_specs=(P(("grp", "blk"), None, None), P(), P(), P("blk", None, None), P("blk", None)),
        out_specs=(P("blk", "grp", None), P("blk", "grp", None)),
        check_vma=False,
    )
```
